256 devices in a mesh: section: 4 (over y_hi, core), tok: 16 (over z, y_lo), lat: 4 (over x).
Axes of the slice: x: 4, y: 4 (y_hi: 2, y_lo: 2; y = y_hi * 2 + y_lo), z: 8, core: 2. Of those that a mesh axis runs over, the one named last changes fastest.
Arguments:
- resid: bfloat16 [4, 2048, 4608], P('section', 'tok', 'lat'), may hold values from -6 to 6
- block_lists: int32 [4, 64, 32], P('section'), may hold values from 0 to 255, all different within a row; in each aligned block of 64 rows (0 to 63, 64 to 127, ..., all dimensions but the last counted through in order) at most 20 rows name the same one
- threshold_level: int32 [4, 32768], P('section', 'tok'), may hold values from 0 to 8
- w_enc: bfloat16 [4, 4608, 32768], P('section', 'lat', 'tok'), may hold values from -0.09375 to 0.09375
- w_dec: bfloat16 [4, 32768, 4608], P('section', 'tok', 'lat'), may hold values from -0.09375 to 0.09375
Outputs:
- reconstruction: bfloat16 [2048, 4608], P(('section', 'tok'), 'lat')
The draws below stay inside these ranges and needn't reach their ends.
Inputs may be any that keep to these rules, and one draw needn't show every extreme that they name: `block_lists`: each row lists 32 different blocks. Within one source layer no block is named by more than 20 tiles, and some block is named by exactly 20 tiles.
All inputs are finite; a program needn't handle non-finite values.
Results may differ from the reference program's by a relative error of at most 0.0049.
Values may be sent and summed in bfloat16 or wider, within the bound.
No kernel may reach another device: no remote copies, remote signals or barrier semaphores. Data moves between devices by JAX's collectives and lax.ppermute only.
A program may use at most 128 MiB of HBM per device.

```python
import math
import jax
import jax.numpy as jnp
import numpy as np
from jax import lax

D = 4608
BLOCK = 128
K_ACT = 32
TILE = 32
TILES = 64
TOKENS = 2048
NB = 256
LATENTS = 32768
SRC = 4
CAPACITY = 20


def touch_ends(result, key, least, largest):
    index_at = [jax.random.randint(jax.random.fold_in(key, axis), (), 0, length) for axis, length in enumerate(result.shape)]
    main_axis = result.shape.index(max(result.shape))
    neighbour = index_at[:main_axis] + [(index_at[main_axis] + 1) % result.shape[main_axis]] + index_at[main_axis + 1:]
    return result.at[tuple(index_at)].set(least).at[tuple(neighbour)].set(largest)


def shard_levels(rng, extent, cuts, smallest, top_value):
    gain, own = 1.0, jax.random.fold_in(rng, 6)
    for position, blocks in cuts:
        draws = jnp.exp(jax.random.uniform(jax.random.fold_in(own, position), (blocks,), jnp.float32, smallest / len(cuts), top_value / len(cuts)))
        gain = gain * jnp.repeat(draws, extent[position] // blocks).reshape([-1 if axis == position else 1 for axis in range(len(extent))])
    return gain


def assign_block(key, own, number, rows, amount, top, bound, lean):
    ranking = jax.random.permutation(key, amount)
    packed, common = portions_of(amount, rows * top, bound, lean, True), portions_of(amount, rows * top, bound, lean, False)
    places = jnp.arange(amount)

    def named(tallies, offset_by):
        used = int((tallies > 0).sum())
        fixed = max(1, used // 4)
        moved = fixed + (places - fixed + offset_by * (used - fixed)) % max(1, amount - fixed)
        return jnp.zeros((amount,), jnp.int32).at[ranking[jnp.where(places < fixed, places, moved)]].set(jnp.asarray(tallies, jnp.int32))

    tallies = jnp.where(number % 4 == 0, named(packed, number // 4), named(common, number - number // 4 - 1))
    mixed = jax.random.permutation(jax.random.fold_in(own, 3), amount)
    donor, receiver = mixed[0:amount // 2 * 2:2], mixed[1:amount // 2 * 2:2]
    margin = jnp.minimum(tallies[donor] - 1, bound - tallies[receiver]) // 2
    margin = jnp.where((donor == ranking[0]) | (receiver == ranking[0]) | (tallies[receiver] == 0), 0, jnp.maximum(margin, 0))
    moved = jax.random.randint(jax.random.fold_in(own, 4), (amount // 2,), 0, 1 << 20) % (margin + 1)
    tallies = tallies.at[donor].add(-moved).at[receiver].add(moved)
    items = jnp.searchsorted(jnp.cumsum(tallies), jnp.arange(rows * top), side="right").astype(jnp.int32)
    listing = items.reshape(top, rows).T
    listing = listing[jax.random.permutation(jax.random.fold_in(own, 1), rows)]
    offset_by = jax.random.randint(jax.random.fold_in(own, 2), (rows, 1), 0, top)
    return jnp.take_along_axis(listing, (jnp.arange(top)[None, :] + offset_by) % top, axis=1)


def portions_of(count, total, limit, lean, full):
    portions = [(1 << 20) // math.isqrt(standing ** lean) + 1 for standing in range(1, count + 1)]
    largest = limit if full else min(limit, max(-(-total // count), total * portions[0] // sum(portions)))
    least = 1 if total - largest >= count - 1 else 0
    holding, spare = [largest] + [least] * (count - 1), total - largest - least * (count - 1)
    while spare > 0:
        candidates = [i for i in range(1, count) if holding[i] < largest] or [i for i in range(1, count) if holding[i] < limit]
        pool, left = sum([portions[i] for i in candidates]), spare
        for i in candidates:
            addition = min(limit - holding[i], max(1, left * portions[i] // pool), spare)
            holding[i] = holding[i] + addition
            spare = spare - addition
    return np.array(holding)


def normal_values(rng, shape, spread, limit, split=(), dtype=jnp.bfloat16):
    drawn = jax.random.normal(rng, shape, jnp.float32) * spread
    if len(split) > 0:
        drawn = shard_levels(rng, shape, split, -0.22, 0.18) * drawn
    return jnp.clip(drawn, min=-limit, max=limit).astype(dtype)


def setup_inputs(seed: int = 0) -> dict:
    streams_of = jax.random.split(jax.random.key(seed), 6)
    resid = normal_values(streams_of[0], (SRC, TOKENS, D), 1.0, 6.0, ((0, 4), (1, 16), (2, 4)))
    block_lists_keys = jax.random.split(jax.random.fold_in(streams_of[1], 1), SRC * TILES // TILES)
    block_lists_turns = jax.random.permutation(jax.random.fold_in(streams_of[1], 3), SRC * TILES // TILES)
    block_lists = jax.vmap(lambda own, number: assign_block(jax.random.fold_in(streams_of[1], 2), own, number, TILES, NB, K_ACT, CAPACITY, 2))(block_lists_keys, block_lists_turns).reshape((SRC, TILES, K_ACT))
    threshold_level = touch_ends(jax.random.randint(streams_of[2], (SRC, LATENTS), 0, 9), jax.random.fold_in(streams_of[2], 1), 0, 8).astype(jnp.int32)
    w_enc = normal_values(streams_of[3], (SRC, D, LATENTS), D ** -0.5, 0.09375, ((0, 4), (1, 4), (2, 16)))
    w_dec = normal_values(streams_of[4], (SRC, LATENTS, D), (K_ACT * BLOCK) ** -0.5, 0.09375, ((0, 4), (1, 16), (2, 4)))
    return {"resid": resid, "block_lists": block_lists, "threshold_level": threshold_level, "w_enc": w_enc, "w_dec": w_dec}


def reference(resid, block_lists, threshold_level, w_enc, w_dec):
    reconstruction = jnp.zeros((TOKENS, D), jnp.float32)
    for source in range(SRC):
        resid_tiles = resid[source].reshape(TILES, TILE, D)
        encoder = w_enc[source].reshape(D, NB, BLOCK)
        decoder = w_dec[source].reshape(NB, BLOCK, D)
        thresholds = (threshold_level[source].astype(jnp.float32) * 0.125).reshape(NB, BLOCK)

        def tile_work(operands):
            tile_resid, block_ids = operands
            columns = jnp.take(encoder, block_ids, axis=1).reshape(D, K_ACT * BLOCK)
            pre_act = jnp.dot(tile_resid, columns, preferred_element_type=jnp.float32)
            limits = thresholds[block_ids].reshape(K_ACT * BLOCK)
            activations = jnp.maximum(pre_act - limits[None, :], 0.0).astype(jnp.bfloat16)
            decoder_rows = decoder[block_ids].reshape(K_ACT * BLOCK, D)
            return jnp.dot(activations, decoder_rows, preferred_element_type=jnp.float32)

        decoded = lax.map(tile_work, (resid_tiles, block_lists[source]))
        reconstruction = reconstruction + decoded.reshape(TOKENS, D)
    return reconstruction.astype(jnp.bfloat16)
```

```python
import functools

import jax
import jax.numpy as jnp
from jax import lax
from jax.experimental import pallas as pl
from jax.experimental.pallas import tpu as pltpu
from jax.sharding import Mesh, PartitionSpec as P

BLOCK = 128
BPO = 16
TILE = 32
TILES = 64
WIDTH = 1152
CAPACITY = 20
GROUP = 4
FAST = 208
SCALE = 16.0
F32 = jnp.float32
BF16 = jnp.bfloat16
VMEM_LIMIT = 48 << 20


def shift(axis, step, size):
    pairs = [(i, (i + step) % size) for i in range(size)]
    return lambda value: lax.ppermute(value, axis, pairs)


def gather_tokens(rows):
    up, down, swap = shift("z", 1, 8), shift("z", -1, 8), shift("yl", 1, 2)
    own, other = {0: rows}, {}
    own[-1], own[1], other[0] = up(own[0]), down(own[0]), swap(own[0])
    own[-2], own[2], other[-1] = up(own[-1]), down(own[1]), swap(own[-1])
    own[-3], own[3], other[1] = up(own[-2]), down(own[2]), swap(own[1])
    own[4], other[2], other[-2] = up(own[-3]), down(other[1]), swap(own[-2])
    other[-3], other[3], other[4] = up(other[-2]), down(other[2]), swap(own[4])
    order = (0, 1, 2, 3, 4, -3, -2, -1)
    return [own[d] for d in order] + [other[d] for d in order]


def make_tables(lists, places, slots):
    y = places["yh"] * 2 + places["yl"]
    tok = places["z"] * 2 + places["yl"]
    block = jnp.arange(BPO, dtype=jnp.int32)
    named = jnp.any(lists[None] == (tok * BPO + block)[:, None, None], axis=2)
    named_f = named.astype(F32)
    tile = jnp.arange(TILES, dtype=jnp.int32)
    before = jnp.dot(named_f, (tile[:, None] < tile[None, :]).astype(F32))
    counts = jnp.sum(named.astype(jnp.int32), axis=1)
    ends = jnp.sum(jnp.where(block[None, :] <= block[:, None], counts[None, :], 0), axis=1)
    starts = ends - counts
    rank = jnp.where(named, before.astype(jnp.int32) + starts[:, None], -1)
    source = ((((tile >> 2) & 1) ^ places["yl"]) * 8 + (((tile >> 3) - places["z"]) & 7)) * 4 + (tile & 3)
    target = (
        ((((tile >> 4) & 1) ^ places["core"]) * 8 + ((((tile >> 1) & 7) - places["z"]) & 7)) * 4
        + ((((tile >> 5) * 2 + (tile & 1)) - y) & 3)
    )
    code = source + 128 * target
    slot = jnp.arange(slots + 2 * GROUP, dtype=jnp.int32)
    hit = rank.reshape(1, -1) == slot[:, None]
    found = jnp.sum(jnp.where(hit, jnp.tile(code, BPO)[None, :], 0), axis=1)
    part = slots // 4
    quarter = slot // part
    row = ((quarter - places["x"]) & 3) * part + slot - quarter * part
    table = found + 16384 * jnp.where(slot < slots, row, slots)
    offsets = jnp.concatenate([jnp.zeros((1,), jnp.int32), ends])
    return table, offsets, ends


def encode_kernel(slots, table, offsets, *refs):
    shards, (w_ref, out_ref, rows, lhs, sem) = refs[:16], refs[16:]
    step = pl.program_id(0)

    @pl.when(step == 0)
    def _():
        copies = [pltpu.make_async_copy(s, rows.at[pl.ds(4 * i, 4)], sem.at[i]) for i, s in enumerate(shards)]
        for c in copies:
            c.start()
        for c in copies:
            c.wait()

    first, last = offsets[step], offsets[step + 1]

    def group(index, carry):
        base = first + index * GROUP
        codes = [table[base + u] for u in range(GROUP)]
        for u in range(GROUP):
            lhs[pl.ds(u * TILE, TILE), :] = rows[codes[u] & 127]
        part = jnp.dot(lhs[...], w_ref[...], preferred_element_type=F32)
        for u in range(GROUP):
            row = jnp.where(base + u < last, codes[u] >> 14, slots)
            out_ref[row] = part[u * TILE : (u + 1) * TILE]
        return carry

    lax.fori_loop(0, (last - first + GROUP - 1) // GROUP, group, 0)


def encode(slots, table, offsets, shards, w_enc):
    return pl.pallas_call(
        functools.partial(encode_kernel, slots),
        out_shape=jax.ShapeDtypeStruct((slots + 1, TILE, BLOCK), F32),
        grid_spec=pltpu.PrefetchScalarGridSpec(
            num_scalar_prefetch=2,
            grid=(BPO,),
            in_specs=[pl.BlockSpec(memory_space=pl.ANY)] * 16
            + [pl.BlockSpec((WIDTH, BLOCK), lambda b, *_: (0, b))],
            out_specs=pl.BlockSpec((slots + 1, TILE, BLOCK), lambda b, *_: (0, 0, 0)),
            scratch_shapes=[
                pltpu.VMEM((TILES, TILE, WIDTH), BF16),
                pltpu.VMEM((GROUP * TILE, WIDTH), BF16),
                pltpu.SemaphoreType.DMA((16,)),
            ],
        ),
        compiler_params=pltpu.CompilerParams(vmem_limit_bytes=VMEM_LIMIT),
        name="encode",
    )(table, offsets, *[s.reshape(4, TILE, WIDTH) for s in shards], w_enc)


def decode_kernel(slots, table, offsets, *refs):
    pieces, (w_ref, mine_ref, theirs_ref, acts, lhs, total, sem) = refs[:4], refs[4:]
    step = pl.program_id(0)

    @pl.when(step == 0)
    def _():
        part = slots // 4
        copies = [pltpu.make_async_copy(p, acts.at[pl.ds(part * i, part)], sem.at[i]) for i, p in enumerate(pieces)]
        for c in copies:
            c.start()
        total[...] = jnp.zeros_like(total)
        for c in copies:
            c.wait()

    first, last = offsets[step], offsets[step + 1]

    def group(index, carry):
        base = first + index * GROUP
        codes = [table[base + u] for u in range(GROUP)]
        for u in range(GROUP):
            row = jnp.where(base + u < last, codes[u] >> 14, 0)
            lhs[pl.ds(u * TILE, TILE), :] = acts[row]
        part = jnp.dot(lhs[...], w_ref[...], preferred_element_type=F32)
        for u in range(GROUP):
            tile = jnp.where(base + u < last, (codes[u] >> 7) & 127, TILES)
            total[tile] += part[u * TILE : (u + 1) * TILE]
        return carry

    lax.fori_loop(0, (last - first + GROUP - 1) // GROUP, group, 0)

    @pl.when(step == BPO - 1)
    def _():
        half = TILES // 2
        mine_ref[...] = total[0:half]
        theirs_ref[...] = total[half:TILES].astype(BF16)


def decode(slots, table, offsets, pieces, w_dec):
    half = (TILES // 2, TILE, WIDTH)
    return pl.pallas_call(
        functools.partial(decode_kernel, slots),
        out_shape=(jax.ShapeDtypeStruct(half, F32), jax.ShapeDtypeStruct(half, BF16)),
        grid_spec=pltpu.PrefetchScalarGridSpec(
            num_scalar_prefetch=2,
            grid=(BPO,),
            in_specs=[pl.BlockSpec(memory_space=pl.ANY)] * 4
            + [pl.BlockSpec((BLOCK, WIDTH), lambda b, *_: (b, 0))],
            out_specs=(
                pl.BlockSpec(half, lambda b, *_: (0, 0, 0)),
                pl.BlockSpec(half, lambda b, *_: (0, 0, 0)),
            ),
            scratch_shapes=[
                pltpu.VMEM((slots, TILE, BLOCK), BF16),
                pltpu.VMEM((GROUP * TILE, BLOCK), BF16),
                pltpu.VMEM((TILES + 1, TILE, WIDTH), F32),
                pltpu.SemaphoreType.DMA((4,)),
            ],
        ),
        compiler_params=pltpu.CompilerParams(vmem_limit_bytes=VMEM_LIMIT),
        name="decode",
    )(table, offsets, *pieces, w_dec)


def local_work(slots, lists, thresholds, w_enc, w_dec, places, *shards):
    right, left, across = shift("x", 1, 4), shift("x", -1, 4), shift("x", 2, 4)
    table, offsets, ends = make_tables(lists, places, slots)
    part = slots // 4
    pre = encode(slots, table, offsets, shards, w_enc)
    quarters = [pre[r * part : (r + 1) * part] for r in range(4)]
    sent = [(q * SCALE).astype(jnp.float16) for q in quarters[1:]]
    got = [right(sent[0]), across(sent[1]), left(sent[2])]
    mine = places["x"] * part + jnp.arange(part, dtype=jnp.int32)
    block = jnp.sum((mine[:, None] >= ends[None, :]).astype(jnp.int32), axis=1)
    pick = (block[:, None] == jnp.arange(BPO, dtype=jnp.int32)[None, :]).astype(F32)
    limits = jnp.dot(pick, thresholds.astype(F32) * 0.125, precision=lax.Precision.HIGHEST)
    summed = quarters[0] + (got[0].astype(F32) + got[1].astype(F32) + got[2].astype(F32)) * (1.0 / SCALE)
    acts = jnp.maximum(summed - limits[:, None, :], 0.0).astype(BF16)
    pieces = [acts, left(acts), across(acts), right(acts)]
    return decode(slots, table, offsets, pieces, w_dec)


def reduce_tokens(mine, theirs):
    up, down = shift("z", 1, 8), shift("z", -1, 8)
    other = shift("core", 1, 2)(theirs)
    mine = mine.reshape(8, 4 * TILE, WIDTH)
    other = other.reshape(8, 4 * TILE, WIDTH)
    own = [mine[d] + other[d].astype(F32) for d in range(8)]
    a = up(own[4].astype(BF16))
    b = down(own[5].astype(BF16))
    a = up((a.astype(F32) + own[3]).astype(BF16))
    b = down((b.astype(F32) + own[6]).astype(BF16))
    a = up((a.astype(F32) + own[2]).astype(BF16))
    b = down((b.astype(F32) + own[7]).astype(BF16))
    a = up((a.astype(F32) + own[1]).astype(BF16))
    column = (a.astype(F32) + b.astype(F32) + own[0]).reshape(4, TILE, WIDTH)
    y = ("yh", "yl")
    got = [shift(y, r, 4)(column[r]) for r in (1, 2, 3)]
    return (column[0] + got[0] + got[1] + got[2]).astype(BF16)


def shards(resid, block_lists, threshold_level, w_enc, w_dec):
    places = {name: lax.axis_index(name) for name in ("yh", "core", "z", "yl", "x")}
    lists = block_lists[0]
    gathered = gather_tokens(resid[0])
    tok = places["z"] * 2 + places["yl"]
    used = jnp.sum((lists // BPO == tok).astype(jnp.int32))
    thresholds = threshold_level[0].reshape(BPO, BLOCK)
    work = [functools.partial(local_work, slots) for slots in (FAST, BPO * CAPACITY)]
    mine, theirs = lax.cond(used <= FAST, work[0], work[1], lists, thresholds, w_enc[0], w_dec[0], places, *gathered)
    return reduce_tokens(mine, theirs)


def solution(mesh):
    section, tok, lat = ("yh", "core"), ("z", "yl"), "x"
    fine = Mesh(mesh.devices.reshape(2, 2, 8, 2, 4), section + tok + (lat,))
    return jax.shard_map(
        shards,
        mesh=fine,
        in_specs=(
            P(section, tok, lat),
            P(section, None, None),
            P(section, tok),
            P(section, lat, tok),
            P(section, tok, lat),
        ),
        out_specs=P(section + tok, lat),
        check_vma=False,
    )
```

```python
import functools

import jax
import jax.numpy as jnp
from jax import lax
from jax.experimental import pallas as pl
from jax.experimental.pallas import tpu as pltpu
from jax.sharding import Mesh, PartitionSpec as P

BLOCK = 128
BPO = 16
TILE = 32
TILES = 64
WIDTH = 1152
SLOTS = 320
GROUP = 8
HALF_GROUP = 4
W_SPLIT = 4
FAST = 208
SCALE = 16.0
F32 = jnp.float32
BF16 = jnp.bfloat16
ENCODE_LIMIT = 20 << 20
DECODE_LIMIT = 24 << 20


def shift(axis, step, size):
    pairs = [(i, (i + step) % size) for i in range(size)]
    return lambda value: lax.ppermute(value, axis, pairs)


def gather_tokens(rows):
    up, down, swap = shift("z", 1, 8), shift("z", -1, 8), shift("yl", 1, 2)
    own, other = {0: rows}, {}
    own[-1], own[1], other[0] = up(own[0]), down(own[0]), swap(own[0])
    own[-2], own[2], other[-1] = up(own[-1]), down(own[1]), swap(own[-1])
    own[-3], own[3], other[1] = up(own[-2]), down(own[2]), swap(own[1])
    own[4], other[2], other[-2] = up(own[-3]), down(other[1]), swap(own[-2])
    other[-3], other[3], other[4] = up(other[-2]), down(other[2]), swap(own[4])
    order = (0, 1, 2, 3, 4, -3, -2, -1)
    return [own[d] for d in order] + [other[d] for d in order]


def make_tables(lists, places):
    y = places["yh"] * 2 + places["yl"]
    tok = places["z"] * 2 + places["yl"]
    block = jnp.arange(BPO, dtype=jnp.int32)
    named = jnp.any(lists[None] == (tok * BPO + block)[:, None, None], axis=2)
    tile = jnp.arange(TILES, dtype=jnp.int32)
    near = ((tile >> 4) & 1) ^ places["core"] ^ 1
    key = near * TILES + tile
    before = jnp.dot(named.astype(F32), (key[:, None] < key[None, :]).astype(F32))
    counts = jnp.sum(named.astype(jnp.int32), axis=1)
    far = jnp.sum(jnp.where(near[None, :] == 0, named.astype(jnp.int32), 0), axis=1)
    ends = jnp.sum(jnp.where(block[None, :] <= block[:, None], counts[None, :], 0), axis=1)
    starts = ends - counts
    rank = jnp.where(named, before.astype(jnp.int32) + starts[:, None], -1)
    source = ((((tile >> 2) & 1) ^ places["yl"]) * 8 + (((tile >> 3) - places["z"]) & 7)) * 4 + (tile & 3)
    target = ((((tile >> 5) * 2 + (tile & 1)) - y) & 3) * 8 + ((((tile >> 1) & 7) - places["z"]) & 7)
    code = source + 128 * target
    slot = jnp.arange(SLOTS + 2 * GROUP, dtype=jnp.int32)
    hit = rank.reshape(1, -1) == slot[:, None]
    found = jnp.sum(jnp.where(hit, jnp.tile(code, BPO)[None, :], 0), axis=1)
    table = found + 16384 * jnp.where(slot < FAST, turned(slot, 0, FAST, places), turned(slot, FAST, SLOTS, places))
    return table, jnp.concatenate([starts, starts + far, ends])


def turned(slot, low, high, places):
    part = (high - low) // 4
    quarter = (slot - low) // part
    return low + ((quarter - places["x"]) & 3) * part + slot - low - quarter * part


def encode_kernel(low, high, table, offsets, *refs):
    shards, (w_hbm, out_ref, rows, w_buf, lhs, sem, w_sem) = refs[:16], refs[16:]
    wide = W_SPLIT * BLOCK
    copies = [pltpu.make_async_copy(s, rows.at[pl.ds(4 * i, 4)], sem.at[i]) for i, s in enumerate(shards)]
    loads = [
        pltpu.make_async_copy(w_hbm.at[:, pl.ds(i * wide, wide)], w_buf.at[i], w_sem.at[i])
        for i in range(BPO // W_SPLIT)
    ]
    for c in copies + loads:
        c.start()
    for c in copies + loads:
        c.wait()

    def block(index, carry):
        first = jnp.maximum(offsets[index], low)
        last = jnp.minimum(offsets[2 * BPO + index], high)
        outer = index // W_SPLIT
        column = pl.ds(pl.multiple_of((index - outer * W_SPLIT) * BLOCK, BLOCK), BLOCK)

        def group(g, carry):
            base = first + g * GROUP
            codes = [table[base + u] for u in range(GROUP)]
            for u in range(GROUP):
                lhs[pl.ds(u * TILE, TILE), :] = rows[codes[u] & 127]
            part = jnp.dot(lhs[...], w_buf[outer, :, column], preferred_element_type=F32)
            for u in range(GROUP):
                row = jnp.where(base + u < last, (codes[u] >> 14) - low, high - low)
                out_ref[row] = part[u * TILE : (u + 1) * TILE]
            return carry

        return lax.fori_loop(0, (last - first + GROUP - 1) // GROUP, group, carry)

    lax.fori_loop(0, BPO, block, 0)


def encode(low, high, table, offsets, shards, w_enc):
    return pl.pallas_call(
        functools.partial(encode_kernel, low, high),
        out_shape=jax.ShapeDtypeStruct((high - low + 1, TILE, BLOCK), F32),
        grid_spec=pltpu.PrefetchScalarGridSpec(
            num_scalar_prefetch=2,
            grid=(),
            in_specs=[pl.BlockSpec(memory_space=pl.ANY)] * 17,
            out_specs=pl.BlockSpec(memory_space=pltpu.VMEM),
            scratch_shapes=[
                pltpu.VMEM((TILES, TILE, WIDTH), BF16),
                pltpu.VMEM((BPO // W_SPLIT, WIDTH, W_SPLIT * BLOCK), BF16),
                pltpu.VMEM((GROUP * TILE, WIDTH), BF16),
                pltpu.SemaphoreType.DMA((16,)),
                pltpu.SemaphoreType.DMA((BPO // W_SPLIT,)),
            ],
        ),
        compiler_params=pltpu.CompilerParams(vmem_limit_bytes=ENCODE_LIMIT),
        name="encode",
    )(table, offsets, *[s.reshape(4, TILE, WIDTH) for s in shards], w_enc)


def decode_kernel(near, table, offsets, *refs):
    pieces, (w_hbm, out_ref, acts, w_buf, lhs, total, sem, w_sem) = refs[:8], refs[8:]
    half = TILES // 2
    copies, at = [], 0
    for i, p in enumerate(pieces):
        copies.append(pltpu.make_async_copy(p, acts.at[pl.ds(at, p.shape[0])], sem.at[i]))
        at += p.shape[0]
    lines = BPO * BLOCK // W_SPLIT
    loads = [
        pltpu.make_async_copy(w_hbm.at[pl.ds(i * lines, lines)], w_buf.at[pl.ds(i * lines, lines)], w_sem.at[i])
        for i in range(W_SPLIT)
    ]
    for c in copies + loads:
        c.start()
    total[...] = jnp.zeros_like(total)
    for c in copies + loads:
        c.wait()

    def block(index, carry):
        first, last = offsets[near * BPO + index], offsets[(near + 1) * BPO + index]
        line = pl.ds(pl.multiple_of(index * BLOCK, BLOCK), BLOCK)

        def group(g, carry):
            base = first + g * HALF_GROUP
            codes = [table[base + u] for u in range(HALF_GROUP)]
            for u in range(HALF_GROUP):
                row = jnp.where(base + u < last, codes[u] >> 14, 0)
                lhs[pl.ds(u * TILE, TILE), :] = acts[row]
            part = jnp.dot(lhs[...], w_buf[line, :], preferred_element_type=F32)
            for u in range(HALF_GROUP):
                tile = jnp.where(base + u < last, (codes[u] >> 7) & 127, half)
                total[tile] += part[u * TILE : (u + 1) * TILE]
            return carry

        return lax.fori_loop(0, (last - first + HALF_GROUP - 1) // HALF_GROUP, group, carry)

    lax.fori_loop(0, BPO, block, 0)
    out_ref[...] = total[0:half].astype(out_ref.dtype)


def decode(near, table, offsets, pieces, w_dec):
    return pl.pallas_call(
        functools.partial(decode_kernel, near),
        out_shape=jax.ShapeDtypeStruct((TILES // 2, TILE, WIDTH), F32 if near else BF16),
        grid_spec=pltpu.PrefetchScalarGridSpec(
            num_scalar_prefetch=2,
            grid=(),
            in_specs=[pl.BlockSpec(memory_space=pl.ANY)] * 9,
            out_specs=pl.BlockSpec(memory_space=pltpu.VMEM),
            scratch_shapes=[
                pltpu.VMEM((SLOTS, TILE, BLOCK), BF16),
                pltpu.VMEM((BPO * BLOCK, WIDTH), BF16),
                pltpu.VMEM((HALF_GROUP * TILE, BLOCK), BF16),
                pltpu.VMEM((TILES // 2 + 1, TILE, WIDTH), F32),
                pltpu.SemaphoreType.DMA((8,)),
                pltpu.SemaphoreType.DMA((W_SPLIT,)),
            ],
        ),
        compiler_params=pltpu.CompilerParams(vmem_limit_bytes=DECODE_LIMIT),
        name="decode_near" if near else "decode_far",
    )(table, offsets, *pieces, w_dec)


def activate(low, high, table, offsets, thresholds, w_enc, places, *shards):
    right, left, across = shift("x", 1, 4), shift("x", -1, 4), shift("x", 2, 4)
    part = (high - low) // 4
    pre = encode(low, high, table, offsets, shards, w_enc)
    quarters = [pre[r * part : (r + 1) * part] for r in range(4)]
    sent = [(q * SCALE).astype(jnp.float16) for q in quarters[1:]]
    got = [right(sent[0]), across(sent[1]), left(sent[2])]
    mine = low + places["x"] * part + jnp.arange(part, dtype=jnp.int32)
    block = jnp.sum((mine[:, None] >= offsets[None, 2 * BPO :]).astype(jnp.int32), axis=1)
    pick = (block[:, None] == jnp.arange(BPO, dtype=jnp.int32)[None, :]).astype(F32)
    limits = jnp.dot(pick, thresholds.astype(F32) * 0.125, precision=lax.Precision.HIGHEST)
    summed = quarters[0] + (got[0].astype(F32) + got[1].astype(F32) + got[2].astype(F32)) * (1.0 / SCALE)
    acts = jnp.maximum(summed - limits[:, None, :], 0.0).astype(BF16)
    return acts, left(acts), across(acts), right(acts)


def no_more(table, offsets, thresholds, w_enc, places, *shards):
    return (jnp.zeros(((SLOTS - FAST) // 4, TILE, BLOCK), BF16),) * 4


def reduce_tokens(mine, other):
    y = ("yh", "yl")
    mine = mine.reshape(4, 8, TILE, WIDTH)
    other = other.reshape(4, 8, TILE, WIDTH)
    sent = [(mine[r] + other[r].astype(F32)).astype(BF16) for r in (2, 1, 3)]
    got = [shift(y, r, 4)(s) for r, s in zip((2, 1, 3), sent)]
    column = mine[0] + other[0].astype(F32) + got[0].astype(F32) + got[1].astype(F32) + got[2].astype(F32)
    ways = (4, 3, 5, 2, 6, 1, 7)
    sent = [column[d].astype(BF16) for d in ways]
    got = [shift("z", d, 8)(s) for d, s in zip(ways, sent)]
    result = column[0]
    for g in got:
        result = result + g.astype(F32)
    return result.astype(BF16)


def shards(resid, block_lists, threshold_level, w_enc, w_dec):
    places = {name: lax.axis_index(name) for name in ("yh", "core", "z", "yl", "x")}
    table, offsets = make_tables(block_lists[0], places)
    gathered = gather_tokens(resid[0])
    operands = (table, offsets, threshold_level[0].reshape(BPO, BLOCK), w_enc[0], places, *gathered)
    pieces = activate(0, FAST, *operands)
    more = lax.cond(offsets[3 * BPO - 1] > FAST, functools.partial(activate, FAST, SLOTS), no_more, *operands)
    pieces = pieces + tuple(more)
    other = shift("core", 1, 2)(decode(0, table, offsets, pieces, w_dec[0]))
    return reduce_tokens(decode(1, table, offsets, pieces, w_dec[0]), other)


def solution(mesh):
    section, tok, lat = ("yh", "core"), ("z", "yl"), "x"
    fine = Mesh(mesh.devices.reshape(2, 2, 8, 2, 4), section + tok + (lat,))
    return jax.shard_map(
        shards,
        mesh=fine,
        in_specs=(
            P(section, tok, lat),
            P(section, None, None),
            P(section, tok),
            P(section, lat, tok),
            P(section, tok, lat),
        ),
        out_specs=P(section + tok, lat),
        check_vma=False,
    )
```

```python
import functools

import jax
import jax.numpy as jnp
from jax import lax
from jax.experimental import pallas as pl
from jax.experimental.pallas import tpu as pltpu
from jax.sharding import Mesh, PartitionSpec as P

BLOCK = 128
BPO = 16
TILE = 32
TILES = 64
WIDTH = 1152
LATENTS = BPO * BLOCK
SLOTS = 320
FAST = 208
EARLY = 10
GROUP = 8
UNROLL = 4
SCALE = 16.0
F32 = jnp.float32
BF16 = jnp.bfloat16
Y = ("yh", "yl")
Y_WAYS = (2, 1, 3)


def shift(axis, step, size):
    pairs = [(i, (i + step) % size) for i in range(size)]
    return lambda value: lax.ppermute(value, axis, pairs)


ARRIVALS = (
    (0, 0), (0, 1), (0, -1), (0, 2), (0, -2), (0, 3), (0, -3), (1, 0), (1, -1), (1, 1),
    (0, 4), (1, 2), (1, -2), (1, 3), (1, -3), (1, 4),
)


def gather_tokens(rows):
    up, down, swap = shift("z", 1, 8), shift("z", -1, 8), shift("yl", 1, 2)
    own, other = {0: rows}, {}
    own[-1], own[1], other[0] = up(own[0]), down(own[0]), swap(own[0])
    own[-2], own[2], other[-1] = up(own[-1]), down(own[1]), swap(own[-1])
    own[-3], own[3], other[1] = up(own[-2]), down(own[2]), swap(own[1])
    own[4], other[2], other[-2] = up(own[-3]), down(other[1]), swap(own[-2])
    other[-3], other[3], other[4] = up(other[-2]), down(other[2]), swap(own[4])
    return [(own, other)[column][distance] for column, distance in ARRIVALS]


def make_table(lists, places):
    y = places["yh"] * 2 + places["yl"]
    tok = places["z"] * 2 + places["yl"]
    block = jnp.arange(BPO, dtype=jnp.int32)
    tile = jnp.arange(TILES, dtype=jnp.int32)
    column = ((tile >> 2) & 1) ^ places["yl"]
    distance = ((tile >> 3) - places["z"]) & 7
    shard = sum(
        jnp.where((column == c) & (distance == d % 8), i, 0) for i, (c, d) in enumerate(ARRIVALS)
    )
    source = shard * 4 + (tile & 3)
    named = jnp.any(lists[None] == (tok * BPO + block)[:, None, None], axis=2)
    before = jnp.dot(named.astype(F32), (source[:, None] < source[None, :]).astype(F32))
    counts = jnp.sum(named.astype(jnp.int32), axis=1)
    early = jnp.sum((named & (source < 4 * EARLY)[None, :]).astype(jnp.int32), axis=1)
    ends = jnp.sum(jnp.where(block[None, :] <= block[:, None], counts[None, :], 0), axis=1)
    starts = ends - counts
    rank = jnp.where(named, before.astype(jnp.int32) + starts[:, None], -1)
    far = ((tile >> 4) & 1) ^ places["core"]
    target = (1 - far) * 32 + ((((tile >> 5) * 2 + (tile & 1)) - y) & 3) * 8 + ((tile >> 1) & 7)
    code = (source + 1024 * target)[None, :] + 64 * block[:, None]
    slot = jnp.arange(SLOTS, dtype=jnp.int32)
    hit = rank.reshape(1, -1) == slot[:, None]
    found = jnp.sum(jnp.where(hit, code.reshape(1, -1), 0), axis=1)
    row = jnp.where(slot < FAST, turned(slot, 0, FAST, places), turned(slot, FAST, SLOTS, places))
    facts = jnp.concatenate([starts, starts + early, ends, jnp.stack([ends[BPO - 1], places["x"]])])
    return found + 65536 * row, facts


def turned(slot, low, high, places):
    part = (high - low) // 4
    quarter = (slot - low) // part
    return low + ((quarter - places["x"]) & 3) * part + slot - low - quarter * part


def encode_kernel(count, lead, bounds, low, high, table, facts, *refs):
    shards, w_ref, refs = refs[:count], refs[count], refs[count + 1 :]
    earlier, (out_ref, rows, lhs, sem, back_sem) = refs[:-5], refs[-5:]
    copies = [pltpu.make_async_copy(s, rows.at[pl.ds(4 * i, 4)], sem.at[i]) for i, s in enumerate(shards)]
    copies += [pltpu.make_async_copy(e, out_ref, back_sem) for e in earlier]
    for c in copies:
        c.start()
    for c in copies:
        c.wait()

    def block(index, carry):
        first = jnp.maximum(facts[bounds[0] * BPO + index], low)
        last = jnp.minimum(facts[bounds[1] * BPO + index], high)
        column = pl.ds(pl.multiple_of(index * BLOCK, BLOCK), BLOCK)

        def group(g, carry):
            codes = [table[jnp.minimum(first + g * GROUP + u, last - 1)] for u in range(GROUP)]
            for u in range(GROUP):
                lhs[pl.ds(u * TILE, TILE), :] = rows[(codes[u] & 63) - 4 * lead]
            part = jnp.dot(lhs[...], w_ref[:, column], preferred_element_type=F32)
            for u in range(GROUP):
                out_ref[(codes[u] >> 16) - low] = part[u * TILE : (u + 1) * TILE]
            return carry

        return lax.fori_loop(0, (jnp.maximum(last - first, 0) + GROUP - 1) // GROUP, group, carry)

    lax.fori_loop(0, BPO, block, 0)


def encode(lead, bounds, low, high, table, facts, shards, w_enc, *earlier):
    count = len(shards)
    any_space = pl.BlockSpec(memory_space=pl.ANY)
    vmem = pl.BlockSpec(memory_space=pltpu.VMEM)
    return pl.pallas_call(
        functools.partial(encode_kernel, count, lead, bounds, low, high),
        out_shape=jax.ShapeDtypeStruct((high - low, TILE, BLOCK), F32),
        grid_spec=pltpu.PrefetchScalarGridSpec(
            num_scalar_prefetch=2,
            grid=(),
            in_specs=[any_space] * count + [vmem] + [any_space] * len(earlier),
            out_specs=vmem,
            scratch_shapes=[
                pltpu.VMEM((4 * count, TILE, WIDTH), BF16),
                pltpu.VMEM((GROUP * TILE, WIDTH), BF16),
                pltpu.SemaphoreType.DMA((count,)),
                pltpu.SemaphoreType.DMA,
            ],
        ),
        compiler_params=pltpu.CompilerParams(vmem_limit_bytes=20 << 20),
        cost_estimate=pl.CostEstimate(flops=count * 5 * 10**8, bytes_accessed=4 * 10**6, transcendentals=0),
        name="encode",
    )(table, facts, *[s.reshape(4, TILE, WIDTH) for s in shards], w_enc, *earlier)


def place_kernel(table, facts, *refs):
    pieces, dense = refs[:5], refs[5]
    dense[...] = jnp.zeros_like(dense)
    total, x = facts[3 * BPO], facts[3 * BPO + 1]
    part = FAST // 4
    for i, piece in enumerate(pieces):
        if i < 4:
            first = ((x + i) & 3) * part
            last = jnp.minimum(first + part, total)
        else:
            first, last = FAST, total

        def move(g, carry, i=i, piece=piece, first=first, last=last):
            for u in range(UNROLL):
                slot = jnp.minimum(first + g * UNROLL + u, last - 1)
                code = table[slot]
                line = pl.ds(pl.multiple_of(((code >> 10) & 63) * TILE, TILE), TILE)
                lane = pl.ds(pl.multiple_of(((code >> 6) & 15) * BLOCK, BLOCK), BLOCK)
                dense[line, lane] = piece[slot - first if i < 4 else (code >> 16) - FAST]
            return carry

        lax.fori_loop(0, (jnp.maximum(last - first, 0) + UNROLL - 1) // UNROLL, move, 0)


def place(table, facts, pieces):
    vmem = pl.BlockSpec(memory_space=pltpu.VMEM)
    return pl.pallas_call(
        place_kernel,
        out_shape=jax.ShapeDtypeStruct((TILES * TILE, LATENTS), BF16),
        grid_spec=pltpu.PrefetchScalarGridSpec(
            num_scalar_prefetch=2, grid=(), in_specs=[vmem] * 5, out_specs=vmem
        ),
        compiler_params=pltpu.CompilerParams(vmem_limit_bytes=16 << 20),
        cost_estimate=pl.CostEstimate(flops=10**6, bytes_accessed=8 * 10**6, transcendentals=0),
        name="place",
    )(table, facts, *pieces)


def activate(low, high, pre, table, thresholds, places):
    right, left, across = shift("x", 1, 4), shift("x", -1, 4), shift("x", 2, 4)
    part = (high - low) // 4
    quarters = [pre[r * part : (r + 1) * part] for r in range(4)]
    sent = [(q * SCALE).astype(jnp.float16) for q in quarters[1:]]
    got = [right(sent[0]), across(sent[1]), left(sent[2])]
    block = (lax.dynamic_slice(table, (low + places["x"] * part,), (part,)) >> 6) & 15
    pick = (block[:, None] == jnp.arange(BPO, dtype=jnp.int32)[None, :]).astype(F32)
    limits = jnp.dot(pick, thresholds.astype(F32) * 0.125, precision=lax.Precision.HIGHEST)
    summed = quarters[0] + (got[0].astype(F32) + got[1].astype(F32) + got[2].astype(F32)) * (1.0 / SCALE)
    acts = jnp.maximum(summed - limits[:, None, :], 0.0).astype(BF16)
    return acts, left(acts), across(acts), right(acts)


def some_more(table, facts, thresholds, w_enc, places, *shards):
    pre = encode(0, (0, 2), FAST, SLOTS, table, facts, shards, w_enc)
    return jnp.concatenate(activate(FAST, SLOTS, pre, table, thresholds, places))


def no_more(table, facts, thresholds, w_enc, places, *shards):
    return jnp.zeros((SLOTS - FAST, TILE, BLOCK), BF16)


def reduce_tokens(mine, other):
    mine = mine.reshape(4, 8, TILE, WIDTH)
    other = other.reshape(4, 8, TILE, WIDTH)
    got = [shift(Y, r, 4)((mine[r] + other[r].astype(F32)).astype(BF16)) for r in Y_WAYS]
    column = mine[0] + other[0].astype(F32) + got[0].astype(F32) + got[1].astype(F32) + got[2].astype(F32)
    got = lax.all_to_all(column.astype(BF16), "z", 0, 0, tiled=True)
    return jnp.sum(got.astype(F32), axis=0).astype(BF16)


def shards(resid, block_lists, threshold_level, w_enc, w_dec):
    places = {name: lax.axis_index(name) for name in ("yh", "core", "z", "yl", "x")}
    w_enc, w_dec = w_enc[0], w_dec[0]
    thresholds = threshold_level[0].reshape(BPO, BLOCK)
    table, facts = make_table(block_lists[0], places)
    gathered = gather_tokens(resid[0])
    if EARLY:
        pre = encode(0, (0, 1), 0, FAST, table, facts, gathered[:EARLY], w_enc)
        pre = encode(EARLY, (1, 2), 0, FAST, table, facts, gathered[EARLY:], w_enc, pre)
    else:
        pre = encode(0, (0, 2), 0, FAST, table, facts, gathered, w_enc)
    pieces = activate(0, FAST, pre, table, thresholds, places)
    more = lax.cond(facts[3 * BPO] > FAST, some_more, no_more, table, facts, thresholds, w_enc, places, *gathered)
    acts = place(table, facts, pieces + (more,))
    half = TILES * TILE // 2
    theirs = jnp.dot(acts[:half], w_dec, preferred_element_type=F32).astype(BF16)
    other = shift("core", 1, 2)(theirs)
    acts, theirs = lax.optimization_barrier((acts, theirs))
    mine = jnp.dot(acts[half:], w_dec, preferred_element_type=F32)
    return reduce_tokens(mine, other)


def solution(mesh):
    section, tok, lat = ("yh", "core"), ("z", "yl"), "x"
    fine = Mesh(mesh.devices.reshape(2, 2, 8, 2, 4), section + tok + (lat,))
    return jax.shard_map(
        shards,
        mesh=fine,
        in_specs=(
            P(section, tok, lat),
            P(section, None, None),
            P(section, tok),
            P(section, lat, tok),
            P(section, tok, lat),
        ),
        out_specs=P(section + tok, lat),
        check_vma=False,
    )
```

```python
import functools

import jax
import jax.numpy as jnp
from jax import lax
from jax.experimental import pallas as pl
from jax.experimental.pallas import tpu as pltpu
from jax.sharding import Mesh, PartitionSpec as P

BLOCK = 128
BPO = 16
TILE = 32
TILES = 64
WIDTH = 1152
LATENTS = BPO * BLOCK
SLOTS = 320
FAST = 208
EARLY = 10
GROUP = 8
UNROLL = 4
SCALE = 16.0
F32 = jnp.float32
BF16 = jnp.bfloat16
Y = ("yh", "yl")
Y_WAYS = (2, 1, 3, 0)


def shift(axis, step, size):
    pairs = [(i, (i + step) % size) for i in range(size)]
    return lambda value: lax.ppermute(value, axis, pairs)


ARRIVALS = (
    (0, 0), (0, 1), (0, -1), (0, 2), (0, -2), (0, 3), (0, -3), (1, 0), (1, -1), (1, 1),
    (0, 4), (1, 2), (1, -2), (1, 3), (1, -3), (1, 4),
)


def gather_tokens(rows, early_work):
    up, down, swap = shift("z", 1, 8), shift("z", -1, 8), shift("yl", 1, 2)
    own, other = {0: rows}, {}
    own[-1], own[1], other[0] = up(own[0]), down(own[0]), swap(own[0])
    own[-2], own[2], other[-1] = up(own[-1]), down(own[1]), swap(own[-1])
    own[-3], own[3], other[1] = up(own[-2]), down(own[2]), swap(own[1])
    own[4], other[2], other[-2] = up(own[-3]), down(other[1]), swap(own[-2])
    early = early_work([(own, other)[column][distance] for column, distance in ARRIVALS[:EARLY]])
    early, own[4], other[2], other[-2] = lax.optimization_barrier((early, own[4], other[2], other[-2]))
    other[-3], other[3], other[4] = up(other[-2]), down(other[2]), swap(own[4])
    return [(own, other)[column][distance] for column, distance in ARRIVALS], early


def make_table(lists, places):
    y = places["yh"] * 2 + places["yl"]
    tok = places["z"] * 2 + places["yl"]
    block = jnp.arange(BPO, dtype=jnp.int32)
    tile = jnp.arange(TILES, dtype=jnp.int32)
    column = ((tile >> 2) & 1) ^ places["yl"]
    distance = ((tile >> 3) - places["z"]) & 7
    shard = sum(
        jnp.where((column == c) & (distance == d % 8), i, 0) for i, (c, d) in enumerate(ARRIVALS)
    )
    source = shard * 4 + (tile & 3)
    named = jnp.any(lists[None] == (tok * BPO + block)[:, None, None], axis=2)
    before = jnp.dot(named.astype(F32), (source[:, None] < source[None, :]).astype(F32))
    counts = jnp.sum(named.astype(jnp.int32), axis=1)
    early = jnp.sum((named & (source < 4 * EARLY)[None, :]).astype(jnp.int32), axis=1)
    ends = jnp.sum(jnp.where(block[None, :] <= block[:, None], counts[None, :], 0), axis=1)
    starts = ends - counts
    rank = jnp.where(named, before.astype(jnp.int32) + starts[:, None], -1)
    far = ((tile >> 4) & 1) ^ places["core"]
    along_y = (((tile >> 5) * 2 + (tile & 1)) - y) & 3
    stand = sum(jnp.where(along_y == r, i, 0) for i, r in enumerate(Y_WAYS))
    target = (1 - far) * 32 + stand * 8 + ((tile >> 1) & 7)
    code = (source + 1024 * target)[None, :] + 64 * block[:, None]
    slot = jnp.arange(SLOTS, dtype=jnp.int32)
    hit = rank.reshape(1, -1) == slot[:, None]
    found = jnp.sum(jnp.where(hit, code.reshape(1, -1), 0), axis=1)
    row = jnp.where(slot < FAST, turned(slot, 0, FAST, places), turned(slot, FAST, SLOTS, places))
    facts = jnp.concatenate([starts, starts + early, ends, jnp.stack([ends[BPO - 1], places["x"]])])
    return found + 65536 * row, facts


def turned(slot, low, high, places):
    part = (high - low) // 4
    quarter = (slot - low) // part
    return low + ((quarter - places["x"]) & 3) * part + slot - low - quarter * part


def encode_kernel(count, lead, bounds, low, high, table, facts, *refs):
    shards, w_ref, refs = refs[:count], refs[count], refs[count + 1 :]
    earlier, (out_ref, rows, lhs, sem, back_sem) = refs[:-5], refs[-5:]
    copies = [pltpu.make_async_copy(s, rows.at[pl.ds(4 * i, 4)], sem.at[i]) for i, s in enumerate(shards)]
    copies += [pltpu.make_async_copy(e, out_ref, back_sem) for e in earlier]
    for c in copies:
        c.start()
    for c in copies:
        c.wait()

    def block(index, carry):
        first = jnp.maximum(facts[bounds[0] * BPO + index], low)
        last = jnp.minimum(facts[bounds[1] * BPO + index], high)
        column = pl.ds(pl.multiple_of(index * BLOCK, BLOCK), BLOCK)

        def group(g, carry):
            codes = [table[jnp.minimum(first + g * GROUP + u, last - 1)] for u in range(GROUP)]
            for u in range(GROUP):
                lhs[pl.ds(u * TILE, TILE), :] = rows[(codes[u] & 63) - 4 * lead]
            part = jnp.dot(lhs[...], w_ref[:, column], preferred_element_type=F32)
            for u in range(GROUP):
                out_ref[(codes[u] >> 16) - low] = part[u * TILE : (u + 1) * TILE]
            return carry

        return lax.fori_loop(0, (jnp.maximum(last - first, 0) + GROUP - 1) // GROUP, group, carry)

    lax.fori_loop(0, BPO, block, 0)


def encode(lead, bounds, low, high, table, facts, shards, w_enc, *earlier):
    count = len(shards)
    any_space = pl.BlockSpec(memory_space=pl.ANY)
    vmem = pl.BlockSpec(memory_space=pltpu.VMEM)
    return pl.pallas_call(
        functools.partial(encode_kernel, count, lead, bounds, low, high),
        out_shape=jax.ShapeDtypeStruct((high - low, TILE, BLOCK), F32),
        grid_spec=pltpu.PrefetchScalarGridSpec(
            num_scalar_prefetch=2,
            grid=(),
            in_specs=[any_space] * count + [vmem] + [any_space] * len(earlier),
            out_specs=vmem,
            scratch_shapes=[
                pltpu.VMEM((4 * count, TILE, WIDTH), BF16),
                pltpu.VMEM((GROUP * TILE, WIDTH), BF16),
                pltpu.SemaphoreType.DMA((count,)),
                pltpu.SemaphoreType.DMA,
            ],
        ),
        compiler_params=pltpu.CompilerParams(vmem_limit_bytes=20 << 20),
        cost_estimate=pl.CostEstimate(flops=count * 5 * 10**8, bytes_accessed=4 * 10**6, transcendentals=0),
        name="encode",
    )(table, facts, *[s.reshape(4, TILE, WIDTH) for s in shards], w_enc, *earlier)


def place_kernel(table, facts, *refs):
    pieces, dense = refs[:5], refs[5]
    dense[...] = jnp.zeros_like(dense)
    total, x = facts[3 * BPO], facts[3 * BPO + 1]
    part = FAST // 4
    for i, piece in enumerate(pieces):
        if i < 4:
            first = ((x + i) & 3) * part
            last = jnp.minimum(first + part, total)
        else:
            first, last = FAST, total

        def move(g, carry, i=i, piece=piece, first=first, last=last):
            for u in range(UNROLL):
                slot = jnp.minimum(first + g * UNROLL + u, last - 1)
                code = table[slot]
                line = pl.ds(pl.multiple_of(((code >> 10) & 63) * TILE, TILE), TILE)
                lane = pl.ds(pl.multiple_of(((code >> 6) & 15) * BLOCK, BLOCK), BLOCK)
                dense[line, lane] = piece[slot - first if i < 4 else (code >> 16) - FAST]
            return carry

        lax.fori_loop(0, (jnp.maximum(last - first, 0) + UNROLL - 1) // UNROLL, move, 0)


def place(table, facts, pieces):
    vmem = pl.BlockSpec(memory_space=pltpu.VMEM)
    return pl.pallas_call(
        place_kernel,
        out_shape=jax.ShapeDtypeStruct((TILES * TILE, LATENTS), BF16),
        grid_spec=pltpu.PrefetchScalarGridSpec(
            num_scalar_prefetch=2, grid=(), in_specs=[vmem] * 5, out_specs=vmem
        ),
        compiler_params=pltpu.CompilerParams(vmem_limit_bytes=16 << 20),
        cost_estimate=pl.CostEstimate(flops=10**6, bytes_accessed=8 * 10**6, transcendentals=0),
        name="place",
    )(table, facts, *pieces)


def activate(low, high, pre, table, thresholds, places):
    right, left, across = shift("x", 1, 4), shift("x", -1, 4), shift("x", 2, 4)
    part = (high - low) // 4
    quarters = [pre[r * part : (r + 1) * part] for r in range(4)]
    sent = [(q * SCALE).astype(jnp.float16) for q in quarters[1:]]
    got = [right(sent[0]), across(sent[1]), left(sent[2])]
    block = (lax.dynamic_slice(table, (low + places["x"] * part,), (part,)) >> 6) & 15
    pick = (block[:, None] == jnp.arange(BPO, dtype=jnp.int32)[None, :]).astype(F32)
    limits = jnp.dot(pick, thresholds.astype(F32) * 0.125, precision=lax.Precision.HIGHEST)
    summed = quarters[0] + (got[0].astype(F32) + got[1].astype(F32) + got[2].astype(F32)) * (1.0 / SCALE)
    acts = jnp.maximum(summed - limits[:, None, :], 0.0).astype(BF16)
    return acts, left(acts), across(acts), right(acts)


def some_more(table, facts, thresholds, w_enc, places, *shards):
    pre = encode(0, (0, 2), FAST, SLOTS, table, facts, shards, w_enc)
    return jnp.concatenate(activate(FAST, SLOTS, pre, table, thresholds, places))


def no_more(table, facts, thresholds, w_enc, places, *shards):
    return jnp.zeros((SLOTS - FAST, TILE, BLOCK), BF16)


def reduce_tokens(acts, w_dec):
    half, group = TILES * TILE // 2, 8 * TILE
    chunks = []
    for start, stop in ((0, group), (group, half)):
        theirs = jnp.dot(acts[start:stop], w_dec, preferred_element_type=F32).astype(BF16)
        other = shift("core", 1, 2)(theirs)
        if chunks:
            acts, theirs, chunks[0] = lax.optimization_barrier((acts, theirs, chunks[0]))
        else:
            acts, theirs = lax.optimization_barrier((acts, theirs))
        mine = jnp.dot(acts[half + start : half + stop], w_dec, preferred_element_type=F32)
        acts, mine = lax.optimization_barrier((acts, mine))
        whole = mine + other.astype(F32)
        if not chunks:
            whole = whole.astype(BF16)
        chunks += [whole[i : i + group] for i in range(0, stop - start, group)]
    got = [shift(Y, r, 4)(c.astype(BF16)) for r, c in zip(Y_WAYS[:3], chunks)]
    column = chunks[3] + got[0].astype(F32) + got[1].astype(F32) + got[2].astype(F32)
    got = lax.all_to_all(column.astype(BF16).reshape(8, TILE, WIDTH), "z", 0, 0, tiled=True)
    return jnp.sum(got.astype(F32), axis=0).astype(BF16)


def shards(resid, block_lists, threshold_level, w_enc, w_dec):
    places = {name: lax.axis_index(name) for name in ("yh", "core", "z", "yl", "x")}
    w_enc, w_dec = w_enc[0], w_dec[0]
    thresholds = threshold_level[0].reshape(BPO, BLOCK)
    table, facts = make_table(block_lists[0], places)
    gathered, early = gather_tokens(
        resid[0], lambda arrived: encode(0, (0, 1), 0, FAST, table, facts, arrived, w_enc)
    )
    pre = encode(EARLY, (1, 2), 0, FAST, table, facts, gathered[EARLY:], w_enc, early)
    pieces = activate(0, FAST, pre, table, thresholds, places)
    more = lax.cond(facts[3 * BPO] > FAST, some_more, no_more, table, facts, thresholds, w_enc, places, *gathered)
    acts = place(table, facts, pieces + (more,))
    return reduce_tokens(acts, w_dec)


def solution(mesh):
    section, tok, lat = ("yh", "core"), ("z", "yl"), "x"
    fine = Mesh(mesh.devices.reshape(2, 2, 8, 2, 4), section + tok + (lat,))
    return jax.shard_map(
        shards,
        mesh=fine,
        in_specs=(
            P(section, tok, lat),
            P(section, None, None),
            P(section, tok),
            P(section, lat, tok),
            P(section, tok, lat),
        ),
        out_specs=P(section + tok, lat),
        check_vma=False,
    )
```

```python
import functools

import jax
import jax.numpy as jnp
from jax import lax
from jax.experimental import pallas as pl
from jax.experimental.pallas import tpu as pltpu
from jax.sharding import Mesh, PartitionSpec as P

BLOCK = 128
BPO = 16
TILE = 32
TILES = 64
WIDTH = 1152
LATENTS = BPO * BLOCK
SLOTS = 320
FAST = 208
EARLY = 10
UNROLL = 4
W_WIDE = 512
SCALE = 16.0
F32 = jnp.float32
BF16 = jnp.bfloat16
Y = ("yh", "yl")
Y_WAYS = (2, 1, 3, 0)


def shift(axis, step, size):
    pairs = [(i, (i + step) % size) for i in range(size)]
    return lambda value: lax.ppermute(value, axis, pairs)


ARRIVALS = (
    (0, 0), (0, 1), (0, -1), (0, 2), (0, -2), (0, 3), (0, -3), (1, 0), (1, -1), (1, 1),
    (0, 4), (1, 2), (1, -2), (1, 3), (1, -3), (1, 4),
)


def gather_tokens(rows, early_work):
    up, down, swap = shift("z", 1, 8), shift("z", -1, 8), shift("yl", 1, 2)
    own, other = {0: rows}, {}
    own[-1], own[1], other[0] = up(own[0]), down(own[0]), swap(own[0])
    own[-2], own[2], other[-1] = up(own[-1]), down(own[1]), swap(own[-1])
    own[-3], own[3], other[1] = up(own[-2]), down(own[2]), swap(own[1])
    own[4], other[2], other[-2] = up(own[-3]), down(other[1]), swap(own[-2])
    early = early_work([(own, other)[column][distance] for column, distance in ARRIVALS[:EARLY]])
    early, own[4], other[2], other[-2] = lax.optimization_barrier((early, own[4], other[2], other[-2]))
    other[-3], other[3], other[4] = up(other[-2]), down(other[2]), swap(own[4])
    return [(own, other)[column][distance] for column, distance in ARRIVALS], early


def make_table(lists, places):
    y = places["yh"] * 2 + places["yl"]
    tok = places["z"] * 2 + places["yl"]
    block = jnp.arange(BPO, dtype=jnp.int32)
    tile = jnp.arange(TILES, dtype=jnp.int32)
    column = ((tile >> 2) & 1) ^ places["yl"]
    distance = ((tile >> 3) - places["z"]) & 7
    shard = sum(
        jnp.where((column == c) & (distance == d % 8), i, 0) for i, (c, d) in enumerate(ARRIVALS)
    )
    source = shard * 4 + (tile & 3)
    named = jnp.any(lists[None] == (tok * BPO + block)[:, None, None], axis=2)
    before = jnp.dot(named.astype(F32), (source[:, None] < source[None, :]).astype(F32))
    counts = jnp.sum(named.astype(jnp.int32), axis=1)
    early = jnp.sum((named & (source < 4 * EARLY)[None, :]).astype(jnp.int32), axis=1)
    ends = jnp.sum(jnp.where(block[None, :] <= block[:, None], counts[None, :], 0), axis=1)
    starts = ends - counts
    rank = jnp.where(named, before.astype(jnp.int32) + starts[:, None], -1)
    far = ((tile >> 4) & 1) ^ places["core"]
    along_y = (((tile >> 5) * 2 + (tile & 1)) - y) & 3
    stand = sum(jnp.where(along_y == r, i, 0) for i, r in enumerate(Y_WAYS))
    target = (1 - far) * 32 + stand * 8 + (((tile >> 1) - places["z"]) & 7)
    code = (source + 1024 * target)[None, :] + 64 * block[:, None]
    slot = jnp.arange(SLOTS, dtype=jnp.int32)
    hit = rank.reshape(1, -1) == slot[:, None]
    found = jnp.sum(jnp.where(hit, code.reshape(1, -1), 0), axis=1)
    row = jnp.where(slot < FAST, turned(slot, 0, FAST, places), turned(slot, FAST, SLOTS, places))
    facts = jnp.concatenate([starts, starts + early, ends, jnp.stack([ends[BPO - 1], places["x"]])])
    return found + 65536 * row, facts


def turned(slot, low, high, places):
    part = (high - low) // 4
    quarter = (slot - low) // part
    return low + ((quarter - places["x"]) & 3) * part + slot - low - quarter * part


def encode_kernel(size, count, lead, bounds, low, high, table, facts, *refs):
    shards, w_ref, refs = refs[:count], refs[count], refs[count + 1 :]
    earlier, (out_ref, rows, w_buf, lhs, sem, w_sem, back_sem) = refs[:-7], refs[-7:]
    loads = []
    if not lead:
        loads = [
            pltpu.make_async_copy(w_ref.at[:, pl.ds(i * W_WIDE, W_WIDE)], w_buf.at[i], w_sem.at[i]) for i in range(4)
        ]
    copies = [pltpu.make_async_copy(s, rows.at[pl.ds(4 * i, 4)], sem.at[i]) for i, s in enumerate(shards)]
    copies += [pltpu.make_async_copy(e, out_ref, back_sem) for e in earlier]
    for c in copies + loads:
        c.start()
    for c in copies:
        c.wait()

    def weights(index):
        if lead:
            return w_ref[:, pl.ds(pl.multiple_of(index * BLOCK, BLOCK), BLOCK)]
        return w_buf[index >> 2, :, pl.ds(pl.multiple_of((index & 3) * BLOCK, BLOCK), BLOCK)]

    def block(index, carry):
        if not lead:

            @pl.when(index & 3 == 0)
            def _():
                at = index >> 2
                pltpu.make_async_copy(w_ref.at[:, pl.ds(0, W_WIDE)], w_buf.at[at], w_sem.at[at]).wait()

        first = jnp.maximum(facts[bounds[0] * BPO + index], low)
        last = jnp.minimum(facts[bounds[1] * BPO + index], high)

        def group(g, carry):
            codes = [table[jnp.minimum(first + g * size + u, last - 1)] for u in range(size)]
            for u in range(size):
                lhs[pl.ds(u * TILE, TILE), :] = rows[(codes[u] & 63) - 4 * lead]
            part = jnp.dot(lhs[...], weights(index), preferred_element_type=F32)
            for u in range(size):
                out_ref[(codes[u] >> 16) - low] = part[u * TILE : (u + 1) * TILE]
            return carry

        return lax.fori_loop(0, (jnp.maximum(last - first, 0) + size - 1) // size, group, carry)

    lax.fori_loop(0, BPO, block, 0)


def encode(size, lead, bounds, low, high, table, facts, shards, w_enc, *earlier):
    count = len(shards)
    any_space = pl.BlockSpec(memory_space=pl.ANY)
    vmem = pl.BlockSpec(memory_space=pltpu.VMEM)
    return pl.pallas_call(
        functools.partial(encode_kernel, size, count, lead, bounds, low, high),
        out_shape=jax.ShapeDtypeStruct((high - low, TILE, BLOCK), F32),
        grid_spec=pltpu.PrefetchScalarGridSpec(
            num_scalar_prefetch=2,
            grid=(),
            in_specs=[any_space] * count + [vmem if lead else pl.BlockSpec(memory_space=pltpu.HBM)] + [any_space] * len(earlier),
            out_specs=vmem,
            scratch_shapes=[
                pltpu.VMEM((4 * count, TILE, WIDTH), BF16),
                pltpu.VMEM((8, 128) if lead else (4, WIDTH, W_WIDE), BF16),
                pltpu.VMEM((size * TILE, WIDTH), BF16),
                pltpu.SemaphoreType.DMA((count,)),
                pltpu.SemaphoreType.DMA((4,)),
                pltpu.SemaphoreType.DMA,
            ],
        ),
        compiler_params=pltpu.CompilerParams(vmem_limit_bytes=20 << 20),
        cost_estimate=pl.CostEstimate(flops=count * 5 * 10**8, bytes_accessed=4 * 10**6, transcendentals=0),
        name="encode",
    )(table, facts, *[s.reshape(4, TILE, WIDTH) for s in shards], w_enc, *earlier)


def place_kernel(table, facts, *refs):
    pieces, dense = refs[:5], refs[5]
    dense[...] = jnp.zeros_like(dense)
    total, x = facts[3 * BPO], facts[3 * BPO + 1]
    part = FAST // 4
    for i, piece in enumerate(pieces):
        if i < 4:
            first = ((x + i) & 3) * part
            last = jnp.minimum(first + part, total)
        else:
            first, last = FAST, total

        def move(g, carry, i=i, piece=piece, first=first, last=last):
            for u in range(UNROLL):
                slot = jnp.minimum(first + g * UNROLL + u, last - 1)
                code = table[slot]
                line = pl.ds(pl.multiple_of(((code >> 10) & 63) * TILE, TILE), TILE)
                lane = pl.ds(pl.multiple_of(((code >> 6) & 15) * BLOCK, BLOCK), BLOCK)
                dense[line, lane] = piece[slot - first if i < 4 else (code >> 16) - FAST]
            return carry

        lax.fori_loop(0, (jnp.maximum(last - first, 0) + UNROLL - 1) // UNROLL, move, 0)


def place(table, facts, pieces):
    vmem = pl.BlockSpec(memory_space=pltpu.VMEM)
    return pl.pallas_call(
        place_kernel,
        out_shape=jax.ShapeDtypeStruct((TILES * TILE, LATENTS), BF16),
        grid_spec=pltpu.PrefetchScalarGridSpec(
            num_scalar_prefetch=2, grid=(), in_specs=[vmem] * 5, out_specs=vmem
        ),
        compiler_params=pltpu.CompilerParams(vmem_limit_bytes=16 << 20),
        cost_estimate=pl.CostEstimate(flops=10**6, bytes_accessed=8 * 10**6, transcendentals=0),
        name="place",
    )(table, facts, *pieces)


def activate(low, high, pre, table, thresholds, places):
    right, left, across = shift("x", 1, 4), shift("x", -1, 4), shift("x", 2, 4)
    part = (high - low) // 4
    quarters = [pre[r * part : (r + 1) * part] for r in range(4)]
    sent = [(q * SCALE).astype(jnp.float16) for q in quarters[1:]]
    got = [right(sent[0]), across(sent[1]), left(sent[2])]
    block = (lax.dynamic_slice(table, (low + places["x"] * part,), (part,)) >> 6) & 15
    pick = (block[:, None] == jnp.arange(BPO, dtype=jnp.int32)[None, :]).astype(F32)
    limits = jnp.dot(pick, thresholds.astype(F32) * 0.125, precision=lax.Precision.HIGHEST)
    summed = quarters[0] + (got[0].astype(F32) + got[1].astype(F32) + got[2].astype(F32)) * (1.0 / SCALE)
    acts = jnp.maximum(summed - limits[:, None, :], 0.0).astype(BF16)
    return acts, left(acts), across(acts), right(acts)


def some_more(table, facts, thresholds, w_enc, places, *shards):
    pre = encode(2, 0, (0, 2), FAST, SLOTS, table, facts, shards, w_enc)
    return jnp.concatenate(activate(FAST, SLOTS, pre, table, thresholds, places))


def no_more(table, facts, thresholds, w_enc, places, *shards):
    return jnp.zeros((SLOTS - FAST, TILE, BLOCK), BF16)


def reduce_tokens(acts, w_dec):
    half, group = TILES * TILE // 2, 8 * TILE
    chunks = []
    for start, stop in ((0, group), (group, half)):
        theirs = jnp.dot(acts[start:stop], w_dec, preferred_element_type=F32).astype(BF16)
        other = shift("core", 1, 2)(theirs)
        if chunks:
            acts, theirs, chunks[0] = lax.optimization_barrier((acts, theirs, chunks[0]))
        else:
            acts, theirs = lax.optimization_barrier((acts, theirs))
        mine = jnp.dot(acts[half + start : half + stop], w_dec, preferred_element_type=F32)
        acts, mine = lax.optimization_barrier((acts, mine))
        whole = mine + other.astype(F32)
        if not chunks:
            whole = whole.astype(BF16)
        chunks += [whole[i : i + group] for i in range(0, stop - start, group)]
    got = [shift(Y, r, 4)(c.astype(BF16)) for r, c in zip(Y_WAYS[:3], chunks)]
    column = chunks[3] + got[0].astype(F32) + got[1].astype(F32) + got[2].astype(F32)
    column = column.reshape(8, TILE, WIDTH)
    result = column[0]
    for got in [shift("z", d, 8)(column[d].astype(BF16)) for d in (4, 3, 5, 2, 6, 1, 7)]:
        result = result + got.astype(F32)
    return result.astype(BF16)


def shards(resid, block_lists, threshold_level, w_enc, w_dec):
    places = {name: lax.axis_index(name) for name in ("yh", "core", "z", "yl", "x")}
    w_enc, w_dec = w_enc[0], w_dec[0]
    w_hbm = pltpu.with_memory_space_constraint(w_enc, pltpu.HBM)
    thresholds = threshold_level[0].reshape(BPO, BLOCK)
    table, facts = make_table(block_lists[0], places)
    gathered, early = gather_tokens(
        resid[0], lambda arrived: encode(8, 0, (0, 1), 0, FAST, table, facts, arrived, w_hbm)
    )
    pre = encode(4, EARLY, (1, 2), 0, FAST, table, facts, gathered[EARLY:], w_enc, early)
    pieces = activate(0, FAST, pre, table, thresholds, places)
    more = lax.cond(facts[3 * BPO] > FAST, some_more, no_more, table, facts, thresholds, w_hbm, places, *gathered)
    acts = place(table, facts, pieces + (more,))
    return reduce_tokens(acts, w_dec)


def solution(mesh):
    section, tok, lat = ("yh", "core"), ("z", "yl"), "x"
    fine = Mesh(mesh.devices.reshape(2, 2, 8, 2, 4), section + tok + (lat,))
    return jax.shard_map(
        shards,
        mesh=fine,
        in_specs=(
            P(section, tok, lat),
            P(section, None, None),
            P(section, tok),
            P(section, lat, tok),
            P(section, tok, lat),
        ),
        out_specs=P(section + tok, lat),
        check_vma=False,
    )
```

```python
import functools

import jax
import jax.numpy as jnp
from jax import lax
from jax.experimental import pallas as pl
from jax.experimental.pallas import tpu as pltpu
from jax.sharding import Mesh, PartitionSpec as P

BLOCK = 128
BPO = 16
TILE = 32
TILES = 64
WIDTH = 1152
LATENTS = BPO * BLOCK
SLOTS = 320
FAST = 208
EARLY = 10
GROUP = 8
UNROLL = 4
W_WIDE = 512
SCALE = 16.0
F32 = jnp.float32
BF16 = jnp.bfloat16
Y = ("yh", "yl")
Y_WAYS = (2, 1, 3, 0)


def shift(axis, step, size):
    pairs = [(i, (i + step) % size) for i in range(size)]
    return lambda value: lax.ppermute(value, axis, pairs)


ARRIVALS = (
    (0, 0), (0, 1), (0, -1), (0, 2), (0, -2), (0, 3), (0, -3), (1, 0), (1, -1), (1, 1),
    (0, 4), (1, 2), (1, -2), (1, 3), (1, -3), (1, 4),
)


def gather_tokens(rows, early_work):
    up, down, swap = shift("z", 1, 8), shift("z", -1, 8), shift("yl", 1, 2)
    own, other = {0: rows}, {}
    own[-1], own[1], other[0] = up(own[0]), down(own[0]), swap(own[0])
    own[-2], own[2], other[-1] = up(own[-1]), down(own[1]), swap(own[-1])
    own[-3], own[3], other[1] = up(own[-2]), down(own[2]), swap(own[1])
    own[4], other[2], other[-2] = up(own[-3]), down(other[1]), swap(own[-2])
    early = early_work([(own, other)[column][distance] for column, distance in ARRIVALS[:EARLY]])
    early, own[4], other[2], other[-2] = lax.optimization_barrier((early, own[4], other[2], other[-2]))
    other[-3], other[3], other[4] = up(other[-2]), down(other[2]), swap(own[4])
    return [(own, other)[column][distance] for column, distance in ARRIVALS], early


def make_table(lists, places):
    y = places["yh"] * 2 + places["yl"]
    tok = places["z"] * 2 + places["yl"]
    block = jnp.arange(BPO, dtype=jnp.int32)
    tile = jnp.arange(TILES, dtype=jnp.int32)
    column = ((tile >> 2) & 1) ^ places["yl"]
    distance = ((tile >> 3) - places["z"]) & 7
    shard = sum(
        jnp.where((column == c) & (distance == d % 8), i, 0) for i, (c, d) in enumerate(ARRIVALS)
    )
    source = shard * 4 + (tile & 3)
    named = jnp.any(lists[None] == (tok * BPO + block)[:, None, None], axis=2)
    before = jnp.dot(named.astype(F32), (source[:, None] < source[None, :]).astype(F32))
    counts = jnp.sum(named.astype(jnp.int32), axis=1)
    early = jnp.sum((named & (source < 4 * EARLY)[None, :]).astype(jnp.int32), axis=1)
    ends = jnp.sum(jnp.where(block[None, :] <= block[:, None], counts[None, :], 0), axis=1)
    starts = ends - counts
    rank = jnp.where(named, before.astype(jnp.int32) + starts[:, None], -1)
    far = ((tile >> 4) & 1) ^ places["core"]
    along_y = (((tile >> 5) * 2 + (tile & 1)) - y) & 3
    stand = sum(jnp.where(along_y == r, i, 0) for i, r in enumerate(Y_WAYS))
    target = (1 - far) * 32 + stand * 8 + ((tile >> 1) & 7)
    code = (source + 1024 * target)[None, :] + 64 * block[:, None]
    slot = jnp.arange(SLOTS, dtype=jnp.int32)
    hit = rank.reshape(1, -1) == slot[:, None]
    found = jnp.sum(jnp.where(hit, code.reshape(1, -1), 0), axis=1)
    row = jnp.where(slot < FAST, turned(slot, 0, FAST, places), turned(slot, FAST, SLOTS, places))
    facts = jnp.concatenate([starts, starts + early, ends, jnp.stack([ends[BPO - 1], places["x"]])])
    return found + 65536 * row, facts


def turned(slot, low, high, places):
    part = (high - low) // 4
    quarter = (slot - low) // part
    return low + ((quarter - places["x"]) & 3) * part + slot - low - quarter * part


def encode_kernel(count, lead, bounds, low, high, table, facts, *refs):
    shards, w_ref, refs = refs[:count], refs[count], refs[count + 1 :]
    earlier, (out_ref, rows, w_buf, lhs, sem, w_sem, back_sem) = refs[:-7], refs[-7:]
    loads = []
    if not lead:
        loads = [
            pltpu.make_async_copy(w_ref.at[:, pl.ds(i * W_WIDE, W_WIDE)], w_buf.at[i], w_sem.at[i]) for i in range(4)
        ]
    copies = [pltpu.make_async_copy(s, rows.at[pl.ds(4 * i, 4)], sem.at[i]) for i, s in enumerate(shards)]
    copies += [pltpu.make_async_copy(e, out_ref, back_sem) for e in earlier]
    for c in copies + loads:
        c.start()
    for c in copies:
        c.wait()

    def weights(index):
        if lead:
            return w_ref[:, pl.ds(pl.multiple_of(index * BLOCK, BLOCK), BLOCK)]
        return w_buf[index >> 2, :, pl.ds(pl.multiple_of((index & 3) * BLOCK, BLOCK), BLOCK)]

    def block(index, carry):
        if not lead:

            @pl.when(index & 3 == 0)
            def _():
                at = index >> 2
                pltpu.make_async_copy(w_ref.at[:, pl.ds(0, W_WIDE)], w_buf.at[at], w_sem.at[at]).wait()

        first = jnp.maximum(facts[bounds[0] * BPO + index], low)
        last = jnp.minimum(facts[bounds[1] * BPO + index], high)

        def group(g, carry):
            codes = [table[jnp.minimum(first + g * GROUP + u, last - 1)] for u in range(GROUP)]
            for u in range(GROUP):
                lhs[pl.ds(u * TILE, TILE), :] = rows[(codes[u] & 63) - 4 * lead]
            part = jnp.dot(lhs[...], weights(index), preferred_element_type=F32)
            for u in range(GROUP):
                out_ref[(codes[u] >> 16) - low] = part[u * TILE : (u + 1) * TILE]
            return carry

        return lax.fori_loop(0, (jnp.maximum(last - first, 0) + GROUP - 1) // GROUP, group, carry)

    lax.fori_loop(0, BPO, block, 0)


def encode(lead, bounds, low, high, table, facts, shards, w_enc, *earlier):
    count = len(shards)
    any_space = pl.BlockSpec(memory_space=pl.ANY)
    vmem = pl.BlockSpec(memory_space=pltpu.VMEM)
    return pl.pallas_call(
        functools.partial(encode_kernel, count, lead, bounds, low, high),
        out_shape=jax.ShapeDtypeStruct((high - low, TILE, BLOCK), F32),
        grid_spec=pltpu.PrefetchScalarGridSpec(
            num_scalar_prefetch=2,
            grid=(),
            in_specs=[any_space] * count + [vmem if lead else pl.BlockSpec(memory_space=pltpu.HBM)] + [any_space] * len(earlier),
            out_specs=vmem,
            scratch_shapes=[
                pltpu.VMEM((4 * count, TILE, WIDTH), BF16),
                pltpu.VMEM((8, 128) if lead else (4, WIDTH, W_WIDE), BF16),
                pltpu.VMEM((GROUP * TILE, WIDTH), BF16),
                pltpu.SemaphoreType.DMA((count,)),
                pltpu.SemaphoreType.DMA((4,)),
                pltpu.SemaphoreType.DMA,
            ],
        ),
        compiler_params=pltpu.CompilerParams(vmem_limit_bytes=20 << 20),
        cost_estimate=pl.CostEstimate(flops=count * 5 * 10**8, bytes_accessed=4 * 10**6, transcendentals=0),
        name="encode",
    )(table, facts, *[s.reshape(4, TILE, WIDTH) for s in shards], w_enc, *earlier)


def place_kernel(table, facts, *refs):
    pieces, dense = refs[:5], refs[5]
    dense[...] = jnp.zeros_like(dense)
    total, x = facts[3 * BPO], facts[3 * BPO + 1]
    part = FAST // 4
    for i, piece in enumerate(pieces):
        if i < 4:
            first = ((x + i) & 3) * part
            last = jnp.minimum(first + part, total)
        else:
            first, last = FAST, total

        def move(g, carry, i=i, piece=piece, first=first, last=last):
            for u in range(UNROLL):
                slot = jnp.minimum(first + g * UNROLL + u, last - 1)
                code = table[slot]
                line = pl.ds(pl.multiple_of(((code >> 10) & 63) * TILE, TILE), TILE)
                lane = pl.ds(pl.multiple_of(((code >> 6) & 15) * BLOCK, BLOCK), BLOCK)
                dense[line, lane] = piece[slot - first if i < 4 else (code >> 16) - FAST]
            return carry

        lax.fori_loop(0, (jnp.maximum(last - first, 0) + UNROLL - 1) // UNROLL, move, 0)


def place(table, facts, pieces):
    vmem = pl.BlockSpec(memory_space=pltpu.VMEM)
    return pl.pallas_call(
        place_kernel,
        out_shape=jax.ShapeDtypeStruct((TILES * TILE, LATENTS), BF16),
        grid_spec=pltpu.PrefetchScalarGridSpec(
            num_scalar_prefetch=2, grid=(), in_specs=[vmem] * 5, out_specs=vmem
        ),
        compiler_params=pltpu.CompilerParams(vmem_limit_bytes=16 << 20),
        cost_estimate=pl.CostEstimate(flops=10**6, bytes_accessed=8 * 10**6, transcendentals=0),
        name="place",
    )(table, facts, *pieces)


def activate(low, high, pre, table, thresholds, places):
    right, left, across = shift("x", 1, 4), shift("x", -1, 4), shift("x", 2, 4)
    part = (high - low) // 4
    quarters = [pre[r * part : (r + 1) * part] for r in range(4)]
    sent = [(q * SCALE).astype(jnp.float16) for q in quarters[1:]]
    got = [right(sent[0]), across(sent[1]), left(sent[2])]
    block = (lax.dynamic_slice(table, (low + places["x"] * part,), (part,)) >> 6) & 15
    pick = (block[:, None] == jnp.arange(BPO, dtype=jnp.int32)[None, :]).astype(F32)
    limits = jnp.dot(pick, thresholds.astype(F32) * 0.125, precision=lax.Precision.HIGHEST)
    summed = quarters[0] + (got[0].astype(F32) + got[1].astype(F32) + got[2].astype(F32)) * (1.0 / SCALE)
    acts = jnp.maximum(summed - limits[:, None, :], 0.0).astype(BF16)
    return acts, left(acts), across(acts), right(acts)


def some_more(table, facts, thresholds, w_enc, places, *shards):
    pre = encode(0, (0, 2), FAST, SLOTS, table, facts, shards, w_enc)
    return jnp.concatenate(activate(FAST, SLOTS, pre, table, thresholds, places))


def no_more(table, facts, thresholds, w_enc, places, *shards):
    return jnp.zeros((SLOTS - FAST, TILE, BLOCK), BF16)


def reduce_tokens(acts, w_dec):
    half, group = TILES * TILE // 2, 8 * TILE
    chunks = []
    for start, stop in ((0, group), (group, half)):
        theirs = jnp.dot(acts[start:stop], w_dec, preferred_element_type=F32).astype(BF16)
        other = shift("core", 1, 2)(theirs)
        if chunks:
            acts, theirs, chunks[0] = lax.optimization_barrier((acts, theirs, chunks[0]))
        else:
            acts, theirs = lax.optimization_barrier((acts, theirs))
        mine = jnp.dot(acts[half + start : half + stop], w_dec, preferred_element_type=F32)
        acts, mine = lax.optimization_barrier((acts, mine))
        whole = mine + other.astype(F32)
        if not chunks:
            whole = whole.astype(BF16)
        chunks += [whole[i : i + group] for i in range(0, stop - start, group)]
    got = [shift(Y, r, 4)(c.astype(BF16)) for r, c in zip(Y_WAYS[:3], chunks)]
    column = chunks[3] + got[0].astype(F32) + got[1].astype(F32) + got[2].astype(F32)
    got = lax.all_to_all(column.astype(BF16).reshape(8, TILE, WIDTH), "z", 0, 0, tiled=True)
    return jnp.sum(got.astype(F32), axis=0).astype(BF16)


def shards(resid, block_lists, threshold_level, w_enc, w_dec):
    places = {name: lax.axis_index(name) for name in ("yh", "core", "z", "yl", "x")}
    w_enc, w_dec = w_enc[0], w_dec[0]
    w_hbm = pltpu.with_memory_space_constraint(w_enc, pltpu.HBM)
    thresholds = threshold_level[0].reshape(BPO, BLOCK)
    table, facts = make_table(block_lists[0], places)
    gathered, early = gather_tokens(
        resid[0], lambda arrived: encode(0, (0, 1), 0, FAST, table, facts, arrived, w_hbm)
    )
    pre = encode(EARLY, (1, 2), 0, FAST, table, facts, gathered[EARLY:], w_enc, early)
    pieces = activate(0, FAST, pre, table, thresholds, places)
    more = lax.cond(facts[3 * BPO] > FAST, some_more, no_more, table, facts, thresholds, w_hbm, places, *gathered)
    acts = place(table, facts, pieces + (more,))
    return reduce_tokens(acts, w_dec)


def solution(mesh):
    section, tok, lat = ("yh", "core"), ("z", "yl"), "x"
    fine = Mesh(mesh.devices.reshape(2, 2, 8, 2, 4), section + tok + (lat,))
    return jax.shard_map(
        shards,
        mesh=fine,
        in_specs=(
            P(section, tok, lat),
            P(section, None, None),
            P(section, tok),
            P(section, lat, tok),
            P(section, tok, lat),
        ),
        out_specs=P(section + tok, lat),
        check_vma=False,
    )
```
